256 devices in a mesh: cp: 32 (over x_lo, z, core), tp: 8 (over y, x_hi).
Axes of the slice: x: 4 (x_hi: 2, x_lo: 2; x = x_hi * 2 + x_lo), y: 4, z: 8, core: 2. Of those that a mesh axis runs over, the one named last changes fastest.
Arguments:
- query: bfloat16 [2048, 16384], P(('cp', 'tp')), may hold values from -6 to 6
- fresh_key_rows: bfloat16 [2048, 1024], P(('cp', 'tp')), may hold values from -6 to 6
- fresh_value_rows: bfloat16 [2048, 1024], P(('cp', 'tp')), may hold values from -6 to 6
- cached_key_rows: bfloat16 [16384, 1024], P('cp', 'tp'), may hold values from -6 to 6
- cached_value_rows: bfloat16 [16384, 1024], P('cp', 'tp'), may hold values from -6 to 6
- prefix_len: int32 [1], replicated, may hold values from 8192 to 16384
- stripe_owner: int32 [32], replicated, may hold values from 0 to 31, each once
Outputs:
- attended: bfloat16 [2048, 16384], P('cp', 'tp')
The draws below stay inside these ranges and needn't reach their ends.
Inputs may be any that keep to these rules, and one draw needn't show every extreme that they name: `stripe_owner`: a permutation of 0 to 31.
All inputs are finite; a program needn't handle non-finite values.
Results may differ from the reference program's by a relative error of at most 0.0075.
Values may be sent and summed in bfloat16 or wider, within the bound.
No kernel may reach another device: no remote copies, remote signals or barrier semaphores. Data moves between devices by JAX's collectives and lax.ppermute only.
A program may use at most 64 MiB of HBM per device.

```python
import math
import jax
import jax.numpy as jnp
from jax import lax

QUERY_HEADS = 128
KEY_VALUE_HEADS = 8
HEAD_SIZE = 128
TOK_DEV = 64
NEW_TOKENS = 2048
CACHE_SLOTS = 16384
N_CP = 32


def draw_query(key, part):
    base_offset = jnp.clip(jax.random.normal(jax.random.fold_in(key, 11), (NEW_TOKENS, QUERY_HEADS * HEAD_SIZE), jnp.float32), -6.0, 6.0)
    return base_offset.astype(jnp.bfloat16)


def draw_cached_key_rows(key, part):
    base_offset = jnp.clip(jax.random.normal(jax.random.fold_in(key, 12), (CACHE_SLOTS, KEY_VALUE_HEADS * HEAD_SIZE), jnp.float32), -6.0, 6.0)
    return base_offset.astype(jnp.bfloat16)


def level_of(rng, extent, shards, low, largest):
    def one(dim, parts):
        heights = jax.random.uniform(jax.random.fold_in(jax.random.fold_in(rng, 6), dim), (parts,), jnp.float32, low / len(shards), largest / len(shards))
        return jnp.repeat(jnp.exp(heights), extent[dim] // parts).reshape((-1,) + (1,) * (len(extent) - dim - 1))

    gain = one(*shards[0])
    for cut in shards[1:]:
        gain = gain * one(*cut)
    return gain


def bell_draw(key, shape, width, most, shards=(), kind=jnp.bfloat16):
    values = jax.random.normal(key, shape, jnp.float32) * width
    if len(shards) > 0:
        values = level_of(key, shape, shards, -0.22, 0.18) * values
    return jnp.clip(values, min=-most, max=most).astype(kind)


def setup_inputs(seed: int = 0) -> dict:
    seeds = jax.random.split(jax.random.key(seed), 8)
    query = draw_query(jax.random.fold_in(seeds[7], 71), 0)
    fresh_key_rows = bell_draw(seeds[1], (NEW_TOKENS, KEY_VALUE_HEADS * HEAD_SIZE), 1.0, 6.0, ((0, 256),))
    fresh_value_rows = bell_draw(seeds[2], (NEW_TOKENS, KEY_VALUE_HEADS * HEAD_SIZE), 1.0, 6.0, ((0, 256),))
    cached_key_rows = draw_cached_key_rows(jax.random.fold_in(seeds[7], 71), 0)
    cached_value_rows = bell_draw(seeds[4], (CACHE_SLOTS, KEY_VALUE_HEADS * HEAD_SIZE), 1.0, 6.0, ((0, 32), (1, 8)))
    prefix_len = jax.random.randint(seeds[5], (1,), CACHE_SLOTS // 2, CACHE_SLOTS + 1).astype(jnp.int32)
    stripe_owner = jax.random.permutation(seeds[6], N_CP).astype(jnp.int32)
    return {"query": query, "fresh_key_rows": fresh_key_rows, "fresh_value_rows": fresh_value_rows, "cached_key_rows": cached_key_rows, "cached_value_rows": cached_value_rows, "prefix_len": prefix_len, "stripe_owner": stripe_owner}


NEG = -1.0e30


def reference(query, fresh_key_rows, fresh_value_rows, cached_key_rows, cached_value_rows, prefix_len, stripe_owner):
    group_size = QUERY_HEADS // KEY_VALUE_HEADS
    scale = HEAD_SIZE ** -0.5
    plen = prefix_len[0]
    block_number = math.gcd(NEW_TOKENS, 256)
    block_count = NEW_TOKENS // block_number
    cache_live = jnp.arange(CACHE_SLOTS, dtype=jnp.int32) < plen
    new_index = jnp.arange(NEW_TOKENS, dtype=jnp.int32)
    combined_keys = jnp.concatenate([cached_key_rows.reshape(CACHE_SLOTS, KEY_VALUE_HEADS, HEAD_SIZE), fresh_key_rows.reshape(NEW_TOKENS, KEY_VALUE_HEADS, HEAD_SIZE)], axis=0).transpose(1, 0, 2)
    combined_values = jnp.concatenate([cached_value_rows.reshape(CACHE_SLOTS, KEY_VALUE_HEADS, HEAD_SIZE), fresh_value_rows.reshape(NEW_TOKENS, KEY_VALUE_HEADS, HEAD_SIZE)], axis=0).transpose(1, 0, 2)
    query_head_rows = query.reshape(block_count, block_number, KEY_VALUE_HEADS, group_size, HEAD_SIZE).transpose(2, 0, 1, 3, 4)

    def per_head(inputs):
        queries, keys, values = inputs
        keys32 = keys.astype(jnp.float32)
        values32 = values.astype(jnp.float32)

        def per_block(pair):
            rows, number = pair
            query_index = number * block_number + jnp.arange(block_number, dtype=jnp.int32)
            scores = jnp.einsum("qgd,kd->gqk", rows.astype(jnp.float32), keys32) * scale
            visible = jnp.concatenate([jnp.broadcast_to(cache_live[None, :], (block_number, CACHE_SLOTS)), new_index[None, :] <= query_index[:, None]], axis=1)
            peak = jnp.max(jnp.where(visible, scores, NEG), axis=-1, keepdims=True)
            weights = jnp.where(visible, jnp.exp(scores - peak), 0.0)
            total = jnp.sum(weights, axis=-1, keepdims=True)
            rounded = lax.optimization_barrier(weights.astype(jnp.bfloat16)).astype(jnp.float32)
            result = jnp.einsum("gqk,kd->gqd", rounded, values32) / total
            return result.astype(jnp.bfloat16)

        return lax.map(per_block, (queries, jnp.arange(block_count, dtype=jnp.int32)))

    outputs = lax.map(per_head, (query_head_rows, combined_keys, combined_values))
    natural = outputs.transpose(1, 3, 0, 2, 4).reshape(NEW_TOKENS, QUERY_HEADS * HEAD_SIZE)
    inverse = jnp.argsort(stripe_owner).astype(jnp.int32)
    stripe = TOK_DEV // N_CP
    arranged = natural.reshape(N_CP, N_CP, stripe, QUERY_HEADS * HEAD_SIZE)[:, inverse]
    return arranged.transpose(1, 0, 2, 3).reshape(NEW_TOKENS, QUERY_HEADS * HEAD_SIZE)
```

```python
import functools

import jax
import jax.numpy as jnp
from jax import lax
from jax.experimental import pallas as pl
from jax.experimental.pallas import tpu as pltpu
from jax.sharding import Mesh
from jax.sharding import PartitionSpec as P

HEAD_SIZE = 128
NEG = -1e30
SCALE2 = HEAD_SIZE ** (-0.5) * 1.4426950408889634
GROUP = 4
BLOCK = 512
PAIR = 2 * BLOCK

bf16 = jnp.bfloat16
f32 = jnp.float32


def attend_kernel(n_cached, has_fresh, first, last, rows, heads, *refs):
    info = refs[0]
    at = 1
    cached = refs[at : at + n_cached]
    at += n_cached
    q_ref = refs[at]
    at += 1
    if has_fresh:
        fresh_ref, fresh_mask = refs[at : at + 2]
        at += 2
    if not first:
        m_in, l_in, acc_in = refs[at : at + 3]
        at += 3
    if last:
        keep_ref, send_ref, lse_ref = refs[at : at + 3]
        at += 3
    else:
        m_ref, l_ref, acc_ref = refs[at : at + 3]
        at += 3
    kbuf, vbuf, qbuf, sbuf, pbuf, sems = refs[at : at + 6]
    at += 6
    if last:
        m_ref, l_ref, acc_ref = refs[at : at + 3]
    groups = heads // GROUP
    wide = GROUP * rows
    plen = info[0]

    def copies(i, slot):
        row = pl.multiple_of(slot * BLOCK, BLOCK)
        return (
            pltpu.make_async_copy(
                cached[i].at[pl.ds(0, BLOCK), :], kbuf.at[pl.ds(row, BLOCK), pl.ds(0, HEAD_SIZE)], sems.at[i]
            ),
            pltpu.make_async_copy(cached[i].at[pl.ds(BLOCK, BLOCK), :], vbuf.at[pl.ds(row, BLOCK), :], sems.at[i]),
        )

    def visit(action):
        slot = jnp.int32(0)
        for i in range(n_cached):
            live = info[1 + i] < plen

            @pl.when(live)
            def _(slot=slot, i=i):
                action(i, slot)

            slot = slot + live.astype(jnp.int32)
        return slot

    def begin(i, slot):
        one, two = copies(i, slot)
        one.start()
        two.start()

    used = visit(begin)

    eye = (
        lax.broadcasted_iota(jnp.int32, (rows, HEAD_SIZE), 0) == lax.broadcasted_iota(jnp.int32, (rows, HEAD_SIZE), 1)
    ).astype(bf16)
    for h in range(heads):
        qbuf[pl.ds(h * rows, rows), 0:HEAD_SIZE] = q_ref[:, h * HEAD_SIZE : (h + 1) * HEAD_SIZE]
        qbuf[pl.ds(h * rows, rows), HEAD_SIZE : 2 * HEAD_SIZE] = eye

    def bias(i, slot):
        spot = lax.broadcasted_iota(jnp.int32, (BLOCK, HEAD_SIZE), 0) + info[1 + i]
        kbuf[pl.ds(pl.multiple_of(slot * BLOCK, BLOCK), BLOCK), pl.ds(HEAD_SIZE, HEAD_SIZE)] = jnp.where(
            spot < plen, 0.0, NEG
        ).astype(bf16)

    visit(bias)
    if has_fresh:
        sources, two, per = fresh_ref.shape[0], fresh_ref.shape[1], fresh_ref.shape[2]
        count = sources * per
        base = pl.multiple_of(used * BLOCK, BLOCK)
        kbuf[pl.ds(base, count), pl.ds(0, HEAD_SIZE)] = fresh_ref[:, 0].reshape(count, HEAD_SIZE)
        vbuf[pl.ds(base, count), :] = fresh_ref[:, 1].reshape(count, HEAD_SIZE)
        kbuf[pl.ds(base, count), pl.ds(HEAD_SIZE, HEAD_SIZE)] = fresh_mask[...]
        used = used + count // BLOCK

    @pl.when(lax.rem(used, 2) == 1)
    def _():
        base = pl.multiple_of(used * BLOCK, BLOCK)
        kbuf[pl.ds(base, BLOCK), pl.ds(0, HEAD_SIZE)] = jnp.zeros((BLOCK, HEAD_SIZE), bf16)
        kbuf[pl.ds(base, BLOCK), pl.ds(HEAD_SIZE, HEAD_SIZE)] = jnp.full((BLOCK, HEAD_SIZE), NEG, bf16)
        vbuf[pl.ds(base, BLOCK), :] = jnp.zeros((BLOCK, HEAD_SIZE), bf16)

    pairs = (used + 1) // 2
    if first:
        m_ref[...] = jnp.full_like(m_ref, NEG)
        l_ref[...] = jnp.zeros_like(l_ref)
        acc_ref[...] = jnp.zeros_like(acc_ref)
    else:
        m_ref[...] = m_in[...]
        l_ref[...] = l_in[...]
        acc_ref[...] = acc_in[...]

    def finish(i, slot):
        one, two = copies(i, slot)
        one.wait()
        two.wait()

    visit(finish)

    def qk(g, b):
        q = qbuf[pl.ds(pl.multiple_of(g * wide, wide), wide), :]
        k = kbuf[pl.ds(pl.multiple_of(b * PAIR, PAIR), PAIR), :]
        return lax.dot_general(k, q, (((1,), (1,)), ((), ())), preferred_element_type=f32)

    def soft(g, s):
        m = m_ref[g]
        new = jnp.maximum(m, jnp.max(s, axis=0, keepdims=True))
        factor = jnp.exp2((m - new) * SCALE2)
        p = jnp.exp2((s - new) * SCALE2)
        m_ref[g] = new
        l_ref[g] = l_ref[g] * factor + jnp.sum(p, axis=0, keepdims=True)
        return factor, p.astype(bf16)

    def pv(b, p):
        v = vbuf[pl.ds(pl.multiple_of(b * PAIR, PAIR), PAIR), :]
        return lax.dot_general(v, p, (((0,), (0,)), ((), ())), preferred_element_type=f32)

    def after(g, b):
        end = b + 1 == pairs
        return jnp.where(end, g + 1, g), jnp.where(end, 0, b + 1)

    zero = jnp.int32(0)
    g1, b1 = after(zero, zero)
    sbuf[0] = qk(zero, zero)
    sbuf[1] = qk(g1, b1)
    factor0, p0 = soft(zero, sbuf[0])
    pbuf[0] = p0

    def body(t, carry):
        g0, b0, g, b, factor = carry
        i = lax.rem(t, 2)
        gn, bn = after(g, b)
        s_next = qk(jnp.minimum(gn, groups - 1), bn)
        o = pv(b0, pbuf[1 - i])
        new_factor, p = soft(g, sbuf[i])
        acc_ref[g0] = acc_ref[g0] * factor + o
        pbuf[i] = p
        sbuf[1 - i] = s_next
        return (g, b, gn, bn, new_factor)

    steps = groups * pairs
    g0, b0, _, _, factor = lax.fori_loop(1, steps, body, (zero, zero, g1, b1, factor0))
    o = pv(b0, pbuf[lax.rem(steps - 1, 2)])
    acc_ref[g0] = acc_ref[g0] * factor + o

    if last:
        half = rows // 2
        for g in range(groups):
            total = l_ref[g]
            lse = m_ref[g] * SCALE2 + jnp.log2(total)
            out = (acc_ref[g] / total).T
            for j in range(GROUP):
                h = g * GROUP + j
                piece = out[j * rows : (j + 1) * rows]
                keep_ref[:, h * HEAD_SIZE : (h + 1) * HEAD_SIZE] = piece[:half]
                send_ref[:, h * HEAD_SIZE : (h + 1) * HEAD_SIZE] = piece[half:].astype(bf16)
                lse_ref[h : h + 1, :] = lse[:, j * rows : (j + 1) * rows]


def attend(info, cached, queries, heads, fresh=None, state=None, last=False):
    rows = queries.shape[0]
    wide = GROUP * rows
    groups = heads // GROUP
    first = state is None
    n_cached = len(cached)
    slots = n_cached + (0 if fresh is None else fresh[0].shape[0] * fresh[0].shape[2] // BLOCK)
    slots = slots + slots % 2
    vm = pl.BlockSpec(memory_space=pltpu.VMEM)
    args = [info, *cached, queries]
    specs = [pl.BlockSpec(memory_space=pltpu.SMEM)] + [pl.BlockSpec(memory_space=pl.ANY)] * n_cached + [vm]
    if fresh is not None:
        args += list(fresh)
        specs += [vm, vm]
    if not first:
        args += list(state)
        specs += [vm] * 3
    states = [
        ((groups, 1, wide), f32),
        ((groups, 1, wide), f32),
        ((groups, HEAD_SIZE, wide), f32),
    ]
    if last:
        outs = [
            jax.ShapeDtypeStruct((rows // 2, heads * HEAD_SIZE), f32),
            jax.ShapeDtypeStruct((rows // 2, heads * HEAD_SIZE), bf16),
            jax.ShapeDtypeStruct((heads, rows), f32),
        ]
    else:
        outs = [jax.ShapeDtypeStruct(s, d) for s, d in states]
    scratch = [
        pltpu.VMEM((slots * BLOCK, 2 * HEAD_SIZE), bf16),
        pltpu.VMEM((slots * BLOCK, HEAD_SIZE), bf16),
        pltpu.VMEM((heads * rows, 2 * HEAD_SIZE), bf16),
        pltpu.VMEM((2, PAIR, wide), f32),
        pltpu.VMEM((2, PAIR, wide), bf16),
        pltpu.SemaphoreType.DMA((max(n_cached, 1),)),
    ]
    if last:
        scratch += [pltpu.VMEM(s, d) for s, d in states]
    return pl.pallas_call(
        functools.partial(attend_kernel, n_cached, fresh is not None, first, last, rows, heads),
        out_shape=outs,
        in_specs=specs,
        out_specs=[vm] * 3,
        scratch_shapes=scratch,
        compiler_params=pltpu.CompilerParams(vmem_limit_bytes=40 * 2**20),
        cost_estimate=pl.CostEstimate(
            flops=4 * slots * BLOCK * heads * rows * HEAD_SIZE * 2,
            bytes_accessed=slots * BLOCK * HEAD_SIZE * 4,
            transcendentals=slots * BLOCK * heads * rows,
        ),
    )(*args)


def merge_kernel(heads, keep_ref, got_ref, mine_ref, theirs_ref, out_ref):
    half = keep_ref.shape[0]
    mine = mine_ref[...].T[:half]
    theirs = theirs_ref[...].T[half:]
    peak = jnp.maximum(mine, theirs)
    one = jnp.exp2(mine - peak)
    two = jnp.exp2(theirs - peak)
    total = one + two
    one = one / total
    two = two / total
    for h in range(heads):
        cols = slice(h * HEAD_SIZE, (h + 1) * HEAD_SIZE)
        out_ref[:, cols] = (
            keep_ref[:, cols] * one[:, h : h + 1] + got_ref[:, cols].astype(f32) * two[:, h : h + 1]
        ).astype(bf16)


def merge(heads, keep, got, mine, theirs):
    return pl.pallas_call(
        functools.partial(merge_kernel, heads),
        out_shape=jax.ShapeDtypeStruct(keep.shape, bf16),
        in_specs=[pl.BlockSpec(memory_space=pltpu.VMEM)] * 4,
        out_specs=pl.BlockSpec(memory_space=pltpu.VMEM),
    )(keep, got, mine, theirs)


def shards(query, fresh_key_rows, fresh_value_rows, cached_key_rows, cached_value_rows, prefix_len, stripe_owner):
    nx, nz, nc, ntp = (lax.axis_size(a) for a in ("x", "z", "c", "tp"))
    x, z, c = (lax.axis_index(a) for a in ("x", "z", "c"))
    parts = nx * nz * nc
    up = [(i, (i + 1) % nz) for i in range(nz)]
    down = [(i, (i - 1) % nz) for i in range(nz)]
    swap = [(0, 1), (1, 0)]

    own = jnp.concatenate([cached_key_rows, cached_value_rows], axis=0)
    other = lax.ppermute(own, "x", swap)
    ups, downs = [(own, other)], [(own, other)]
    for _ in range(nz // 2 - 1):
        ups.append(tuple(lax.ppermute(a, "z", up) for a in ups[-1]))
        downs.append(tuple(lax.ppermute(a, "z", down) for a in downs[-1]))
    far_own = lax.ppermute(ups[-1][0], "z", up)
    far_other = lax.ppermute(downs[-1][1], "z", down)

    local = query.shape[0]
    width = query.shape[1] // ntp
    mixed = jnp.concatenate(
        [
            query.reshape(local, ntp, width),
            fresh_key_rows.reshape(local, ntp, HEAD_SIZE),
            fresh_value_rows.reshape(local, ntp, HEAD_SIZE),
        ],
        axis=2,
    ).reshape(local, ntp * (width + 2 * HEAD_SIZE))
    mixed = lax.all_to_all(mixed, "tp", split_axis=1, concat_axis=0, tiled=True)
    rows = mixed.shape[0]
    stripe = rows // parts
    heads = width // HEAD_SIZE
    order = jnp.arange(parts, dtype=jnp.int32)
    inverse = jnp.sum(jnp.where(stripe_owner[None, :] == order[:, None], order[None, :], 0), axis=1)
    row_of = (inverse[:, None] * stripe + jnp.arange(stripe, dtype=jnp.int32)[None, :]).reshape(rows)
    pick = (row_of[:, None] == jnp.arange(rows, dtype=jnp.int32)[None, :]).astype(bf16)
    arranged = jnp.dot(pick, mixed[:, :width], preferred_element_type=f32).astype(bf16)
    mine = lax.all_to_all(arranged, ("x", "z"), split_axis=0, concat_axis=0, tiled=True)
    peers = lax.ppermute(mine, "c", swap)

    def spot(rel, s, src, i):
        part = (src != c).astype(jnp.int32)
        owner = jnp.where(rel == 0, c, 1 - c)
        return part * rows + (s * nc + owner) * stripe + i

    idx = jnp.arange(nc * rows, dtype=jnp.int32)
    i_, src_, s_, rel_ = idx % stripe, idx // stripe % nc, idx // (stripe * nc) % (nx * nz), idx // rows
    choose = (spot(rel_, s_, src_, i_)[:, None] == idx[None, :]).astype(bf16)
    queries = jnp.dot(choose, jnp.concatenate([mine, peers], axis=0), preferred_element_type=f32).astype(bf16)
    owner_ = (x * nz + z) * nc + jnp.where(rel_ == 0, c, 1 - c)
    residue_ = jnp.sum(jnp.where(owner_[:, None] == order[None, :], inverse[None, :], 0), axis=1)
    natural = (s_ * nc + src_) * rows + residue_ * stripe + i_

    fresh = jnp.concatenate(
        [mixed[:, width : width + HEAD_SIZE], mixed[:, width + HEAD_SIZE :]], axis=0
    ).reshape(1, 2, rows, HEAD_SIZE)
    fresh = jnp.broadcast_to(fresh, (nx * nz, 2, rows, HEAD_SIZE))
    fresh = lax.all_to_all(fresh, ("x", "z"), split_axis=0, concat_axis=0, tiled=True)
    key_id = jnp.arange(nx * nz * rows, dtype=jnp.int32)
    key_natural = (key_id // rows * nc + c) * rows + key_id % rows
    fresh_mask = jnp.where(key_natural[:, None] <= natural[None, :], 0.0, NEG).astype(bf16)

    slots = cached_key_rows.shape[0]
    plen = prefix_len[0]

    def start(which_x, step):
        return ((which_x * nz + (z + step + nz) % nz) * nc + c) * slots

    def info_of(where):
        return jnp.stack([plen] + [start(*w) for w in where]).astype(jnp.int32)

    near, near_at = [own, other], [(x, 0), (1 - x, 0)]
    for step in (1, 2):
        near += [*ups[step], *downs[step]]
        near_at += [(x, -step), (1 - x, -step), (x, step), (1 - x, step)]
    mid = [*ups[3], *downs[3]]
    mid_at = [(x, -3), (1 - x, -3), (x, 3), (1 - x, 3)]
    state = attend(info_of(near_at), near, queries, heads)
    state = attend(info_of(mid_at), mid, queries, heads, state=state)
    keep, send, lse = attend(
        info_of([(x, 4), (1 - x, 4)]),
        [far_own, far_other],
        queries,
        heads,
        fresh=(fresh, fresh_mask),
        state=state,
        last=True,
    )
    got = lax.ppermute(send, "c", swap)
    their_lse = lax.ppermute(lse, "c", swap)
    return merge(heads, keep, got, lse, their_lse)


def solution(mesh):
    devices = mesh.devices
    parts = Mesh(devices.reshape(2, devices.shape[0] // 4, 2, devices.shape[1]), ("x", "z", "c", "tp"))
    rows = ("x", "z", "c", "tp")
    cp = ("x", "z", "c")
    return jax.shard_map(
        shards,
        mesh=parts,
        in_specs=(P(rows, None), P(rows, None), P(rows, None), P(cp, "tp"), P(cp, "tp"), P(), P()),
        out_specs=P(cp, "tp"),
        check_vma=False,
    )
```

```python
import functools

import jax
import jax.numpy as jnp
from jax import lax
from jax.experimental import pallas as pl
from jax.experimental.pallas import tpu as pltpu
from jax.sharding import Mesh
from jax.sharding import PartitionSpec as P

HEAD_SIZE = 128
NEG = -1e30
SCALE2 = HEAD_SIZE ** (-0.5) * 1.4426950408889634
GROUP = 8
BLOCK = 512
PARTS = 4

bf16 = jnp.bfloat16
f32 = jnp.float32


def attend_kernel(n_cached, has_fresh, first, last, rows, heads, *refs):
    info = refs[0]
    at = 1
    cached = refs[at : at + n_cached]
    at += n_cached
    q_ref = refs[at]
    at += 1
    if has_fresh:
        fresh_ref, fresh_mask = refs[at : at + 2]
        at += 2
    if not first:
        m_in, l_in, acc_in = refs[at : at + 3]
        at += 3
    if last:
        keep_ref, send_ref, lse_ref = refs[at : at + 3]
        at += 3
    else:
        m_ref, l_ref, acc_ref = refs[at : at + 3]
        at += 3
    kbuf, vbuf, qbuf, s_even, s_odd, p_even, p_odd, sems = refs[at : at + 8]
    at += 8
    if last:
        m_ref, l_ref, acc_ref = refs[at : at + 3]
    groups = heads // GROUP
    wide = GROUP * rows
    plen = info[0]

    def copies(i, slot):
        row = pl.multiple_of(slot * BLOCK, BLOCK)
        return (
            pltpu.make_async_copy(
                cached[i].at[pl.ds(0, BLOCK), :], kbuf.at[pl.ds(row, BLOCK), pl.ds(0, HEAD_SIZE)], sems.at[i]
            ),
            pltpu.make_async_copy(cached[i].at[pl.ds(BLOCK, BLOCK), :], vbuf.at[pl.ds(row, BLOCK), :], sems.at[i]),
        )

    def visit(action):
        slot = jnp.int32(0)
        for i in range(n_cached):
            live = info[1 + i] < plen

            @pl.when(live)
            def _(slot=slot, i=i):
                action(i, slot)

            slot = slot + live.astype(jnp.int32)
        return slot

    def begin(i, slot):
        one, two = copies(i, slot)
        one.start()
        two.start()

    used = visit(begin)

    eye = (
        lax.broadcasted_iota(jnp.int32, (rows, HEAD_SIZE), 0) == lax.broadcasted_iota(jnp.int32, (rows, HEAD_SIZE), 1)
    ).astype(bf16)
    for h in range(heads):
        qbuf[pl.ds(h * rows, rows), 0:HEAD_SIZE] = q_ref[:, h * HEAD_SIZE : (h + 1) * HEAD_SIZE]
        qbuf[pl.ds(h * rows, rows), HEAD_SIZE : 2 * HEAD_SIZE] = eye

    def bias(i, slot):
        spot = lax.broadcasted_iota(jnp.int32, (BLOCK, HEAD_SIZE), 0) + info[1 + i]
        kbuf[pl.ds(pl.multiple_of(slot * BLOCK, BLOCK), BLOCK), pl.ds(HEAD_SIZE, HEAD_SIZE)] = jnp.where(
            spot < plen, 0.0, NEG
        ).astype(bf16)

    visit(bias)
    if has_fresh:
        sources, per = fresh_ref.shape[0], fresh_ref.shape[2]
        count = sources * per
        base = pl.multiple_of(used * BLOCK, BLOCK)
        kbuf[pl.ds(base, count), pl.ds(0, HEAD_SIZE)] = fresh_ref[:, 0].reshape(count, HEAD_SIZE)
        vbuf[pl.ds(base, count), :] = fresh_ref[:, 1].reshape(count, HEAD_SIZE)
        kbuf[pl.ds(base, count), pl.ds(HEAD_SIZE, HEAD_SIZE)] = fresh_mask[...]
        used = used + count // BLOCK

    if first:
        m_ref[...] = jnp.full_like(m_ref, NEG)
        l_ref[...] = jnp.zeros_like(l_ref)
        acc_ref[...] = jnp.zeros_like(acc_ref)
    else:
        m_ref[...] = m_in[...]
        l_ref[...] = l_in[...]
        acc_ref[...] = acc_in[...]

    def finish(i, slot):
        one, two = copies(i, slot)
        one.wait()
        two.wait()

    visit(finish)

    piece = wide // PARTS
    spans = [slice(j * piece, (j + 1) * piece) for j in range(PARTS)]

    def at_block(buf, b):
        return buf[pl.ds(pl.multiple_of(b * BLOCK, BLOCK), BLOCK), :]

    def qk(g, b, j):
        q = qbuf[pl.ds(pl.multiple_of(g * wide + j * piece, piece), piece), :]
        return lax.dot_general(at_block(kbuf, b), q, (((1,), (1,)), ((), ())), preferred_element_type=f32)

    def pv(b, p):
        return lax.dot_general(at_block(vbuf, b), p, (((0,), (0,)), ((), ())), preferred_element_type=f32)

    def after(g, b):
        end = b + 1 == used
        return jnp.where(end, g + 1, g), jnp.where(end, 0, b + 1)

    def turn(carry, s_now, p_now, s_next, p_before):
        g0, b0, old, g, b = carry
        gn, bn = after(g, b)
        factors = []
        for j, span in enumerate(spans):
            s_next[:, span] = qk(jnp.minimum(gn, groups - 1), bn, j)
            s = s_now[:, span]
            m = m_ref[g, :, span]
            new = jnp.maximum(m, jnp.max(s, axis=0, keepdims=True))
            factor = jnp.exp2((m - new) * SCALE2)
            p = jnp.exp2((s - new) * SCALE2)
            m_ref[g, :, span] = new
            l_ref[g, :, span] = l_ref[g, :, span] * factor + jnp.sum(p, axis=0, keepdims=True)
            p_now[:, span] = p.astype(bf16)
            acc_ref[g0, :, span] = acc_ref[g0, :, span] * old[j] + pv(b0, p_before[:, span])
            factors.append(factor)
        return g, b, tuple(factors), gn, bn

    zero = jnp.int32(0)
    p_odd[...] = jnp.zeros_like(p_odd)
    for j, span in enumerate(spans):
        s_even[:, span] = qk(zero, zero, j)

    def body(_, carry):
        carry = turn(carry, s_even, p_even, s_odd, p_odd)
        return turn(carry, s_odd, p_odd, s_even, p_even)

    ones = tuple(jnp.ones((1, piece), f32) for _ in range(PARTS))
    g0, b0, old, _, _ = lax.fori_loop(0, groups * used // 2, body, (zero, zero, ones, zero, zero))
    for j, span in enumerate(spans):
        acc_ref[g0, :, span] = acc_ref[g0, :, span] * old[j] + pv(b0, p_odd[:, span])

    if last:
        half = rows // 2
        for g in range(groups):
            total = l_ref[g]
            lse = m_ref[g] * SCALE2 + jnp.log2(total)
            out = (acc_ref[g] / total).T
            for j in range(GROUP):
                h = g * GROUP + j
                own = out[j * rows : (j + 1) * rows]
                keep_ref[:, h * HEAD_SIZE : (h + 1) * HEAD_SIZE] = own[:half]
                send_ref[:, h * HEAD_SIZE : (h + 1) * HEAD_SIZE] = own[half:].astype(bf16)
                lse_ref[h : h + 1, :] = lse[:, j * rows : (j + 1) * rows]


def attend(info, cached, queries, heads, fresh=None, state=None, last=False):
    rows = queries.shape[0]
    wide = GROUP * rows
    groups = heads // GROUP
    first = state is None
    n_cached = len(cached)
    slots = n_cached + (0 if fresh is None else fresh[0].shape[0] * fresh[0].shape[2] // BLOCK)
    vm = pl.BlockSpec(memory_space=pltpu.VMEM)
    args = [info, *cached, queries]
    specs = [pl.BlockSpec(memory_space=pltpu.SMEM)] + [pl.BlockSpec(memory_space=pl.ANY)] * n_cached + [vm]
    if fresh is not None:
        args += list(fresh)
        specs += [vm, vm]
    if not first:
        args += list(state)
        specs += [vm] * 3
    states = [
        ((groups, 1, wide), f32),
        ((groups, 1, wide), f32),
        ((groups, HEAD_SIZE, wide), f32),
    ]
    if last:
        outs = [
            jax.ShapeDtypeStruct((rows // 2, heads * HEAD_SIZE), f32),
            jax.ShapeDtypeStruct((rows // 2, heads * HEAD_SIZE), bf16),
            jax.ShapeDtypeStruct((heads, rows), f32),
        ]
    else:
        outs = [jax.ShapeDtypeStruct(s, d) for s, d in states]
    scratch = [
        pltpu.VMEM((slots * BLOCK, 2 * HEAD_SIZE), bf16),
        pltpu.VMEM((slots * BLOCK, HEAD_SIZE), bf16),
        pltpu.VMEM((heads * rows, 2 * HEAD_SIZE), bf16),
        pltpu.VMEM((BLOCK, wide), f32),
        pltpu.VMEM((BLOCK, wide), f32),
        pltpu.VMEM((BLOCK, wide), bf16),
        pltpu.VMEM((BLOCK, wide), bf16),
        pltpu.SemaphoreType.DMA((max(n_cached, 1),)),
    ]
    if last:
        scratch += [pltpu.VMEM(s, d) for s, d in states]
    return pl.pallas_call(
        functools.partial(attend_kernel, n_cached, fresh is not None, first, last, rows, heads),
        out_shape=outs,
        in_specs=specs,
        out_specs=[vm] * 3,
        scratch_shapes=scratch,
        compiler_params=pltpu.CompilerParams(vmem_limit_bytes=40 * 2**20),
        cost_estimate=pl.CostEstimate(
            flops=4 * slots * BLOCK * heads * rows * HEAD_SIZE * 2,
            bytes_accessed=slots * BLOCK * HEAD_SIZE * 4,
            transcendentals=slots * BLOCK * heads * rows,
        ),
    )(*args)


def merge_kernel(heads, keep_ref, got_ref, mine_ref, theirs_ref, out_ref):
    half = keep_ref.shape[0]
    mine = mine_ref[...].T[:half]
    theirs = theirs_ref[...].T[half:]
    peak = jnp.maximum(mine, theirs)
    one = jnp.exp2(mine - peak)
    two = jnp.exp2(theirs - peak)
    total = one + two
    one = one / total
    two = two / total
    for h in range(heads):
        cols = slice(h * HEAD_SIZE, (h + 1) * HEAD_SIZE)
        out_ref[:, cols] = (
            keep_ref[:, cols] * one[:, h : h + 1] + got_ref[:, cols].astype(f32) * two[:, h : h + 1]
        ).astype(bf16)


def merge(heads, keep, got, mine, theirs):
    return pl.pallas_call(
        functools.partial(merge_kernel, heads),
        out_shape=jax.ShapeDtypeStruct(keep.shape, bf16),
        in_specs=[pl.BlockSpec(memory_space=pltpu.VMEM)] * 4,
        out_specs=pl.BlockSpec(memory_space=pltpu.VMEM),
    )(keep, got, mine, theirs)


def step(query, fresh_key_rows, fresh_value_rows, cached_key_rows, cached_value_rows, prefix_len, stripe_owner):
    nx, nz, nc, ntp = (lax.axis_size(a) for a in ("x", "z", "c", "tp"))
    x, z, c = (lax.axis_index(a) for a in ("x", "z", "c"))
    parts = nx * nz * nc
    up = [(i, (i + 1) % nz) for i in range(nz)]
    down = [(i, (i - 1) % nz) for i in range(nz)]
    swap = [(0, 1), (1, 0)]

    own = jnp.concatenate([cached_key_rows, cached_value_rows], axis=0)
    other = lax.ppermute(own, "x", swap)

    def hop(above, below):
        return (
            (lax.ppermute(above[0], "z", up), lax.ppermute(above[1], "z", up)),
            (lax.ppermute(below[0], "z", down), lax.ppermute(below[1], "z", down)),
        )

    up1, down1 = hop((own, other), (own, other))
    up2, down2 = hop(up1, down1)

    local = query.shape[0]
    width = query.shape[1] // ntp
    mixed = jnp.concatenate(
        [
            query.reshape(local, ntp, width),
            fresh_key_rows.reshape(local, ntp, HEAD_SIZE),
            fresh_value_rows.reshape(local, ntp, HEAD_SIZE),
        ],
        axis=2,
    ).reshape(local, ntp * (width + 2 * HEAD_SIZE))
    mixed = lax.all_to_all(mixed, "tp", split_axis=1, concat_axis=0, tiled=True)
    rows = mixed.shape[0]
    stripe = rows // parts
    heads = width // HEAD_SIZE
    order = jnp.arange(parts, dtype=jnp.int32)
    inverse = jnp.sum(jnp.where(stripe_owner[None, :] == order[:, None], order[None, :], 0), axis=1)
    row_of = (inverse[:, None] * stripe + jnp.arange(stripe, dtype=jnp.int32)[None, :]).reshape(rows)
    pick = (row_of[:, None] == jnp.arange(rows, dtype=jnp.int32)[None, :]).astype(bf16)
    arranged = jnp.dot(pick, mixed[:, :width], preferred_element_type=f32).astype(bf16)
    mine = lax.all_to_all(arranged, ("x", "z"), split_axis=0, concat_axis=0, tiled=True)
    peers = lax.ppermute(mine, "c", swap)

    def spot(rel, s, src, i):
        part = (src != c).astype(jnp.int32)
        owner = jnp.where(rel == 0, c, 1 - c)
        return part * rows + (s * nc + owner) * stripe + i

    idx = jnp.arange(nc * rows, dtype=jnp.int32)
    i_, src_, s_, rel_ = idx % stripe, idx // stripe % nc, idx // (stripe * nc) % (nx * nz), idx // rows
    choose = (spot(rel_, s_, src_, i_)[:, None] == idx[None, :]).astype(bf16)
    queries = jnp.dot(choose, jnp.concatenate([mine, peers], axis=0), preferred_element_type=f32).astype(bf16)
    owner_ = (x * nz + z) * nc + jnp.where(rel_ == 0, c, 1 - c)
    residue_ = jnp.sum(jnp.where(owner_[:, None] == order[None, :], inverse[None, :], 0), axis=1)
    natural = (s_ * nc + src_) * rows + residue_ * stripe + i_

    fresh = jnp.concatenate(
        [mixed[:, width : width + HEAD_SIZE], mixed[:, width + HEAD_SIZE :]], axis=0
    ).reshape(1, 2, rows, HEAD_SIZE)
    key_id = jnp.arange(nx * nz * rows, dtype=jnp.int32)
    key_natural = (key_id // rows * nc + c) * rows + key_id % rows
    fresh_mask = jnp.where(key_natural[:, None] <= natural[None, :], 0.0, NEG).astype(bf16)

    slots = cached_key_rows.shape[0]

    def info_of(where):
        flip = jnp.array([w[0] for w in where], jnp.int32)
        step = jnp.array([w[1] + nz for w in where], jnp.int32)
        starts = ((jnp.where(flip == 0, x, 1 - x) * nz + (z + step) % nz) * nc + c) * slots
        return jnp.concatenate([prefix_len, starts.astype(jnp.int32)])

    def around(step):
        return [(0, -step), (1, -step), (0, step), (1, step)]

    first_info = info_of([(0, 0), (1, 0)] + around(1))
    state = attend(first_info, [own, other, *up1, *down1], queries, heads)
    up2, down2, state = lax.optimization_barrier((up2, down2, state))
    up3, down3 = hop(up2, down2)
    fresh, state = lax.optimization_barrier((fresh, state))
    fresh = jnp.broadcast_to(fresh, (nx * nz, 2, rows, HEAD_SIZE))
    fresh = lax.all_to_all(fresh, ("x", "z"), split_axis=0, concat_axis=0, tiled=True)
    state = attend(info_of(around(2)), [*up2, *down2], queries, heads, state=state)
    up3, down3, state = lax.optimization_barrier((up3, down3, state))
    far_own = lax.ppermute(up3[0], "z", up)
    far_other = lax.ppermute(down3[1], "z", down)
    state = attend(info_of(around(3)), [*up3, *down3], queries, heads, state=state)
    keep, give, lse = attend(
        info_of([(0, 4), (1, 4)]),
        [far_own, far_other],
        queries,
        heads,
        fresh=(fresh, fresh_mask),
        state=state,
        last=True,
    )
    got = lax.ppermute(give, "c", swap)
    their_lse = lax.ppermute(lse, "c", swap)
    return merge(heads, keep, got, lse, their_lse)


def solution(mesh):
    devices = mesh.devices
    parts = Mesh(devices.reshape(2, devices.shape[0] // 4, 2, devices.shape[1]), ("x", "z", "c", "tp"))
    rows = ("x", "z", "c", "tp")
    cp = ("x", "z", "c")
    return jax.shard_map(
        step,
        mesh=parts,
        in_specs=(P(rows, None), P(rows, None), P(rows, None), P(cp, "tp"), P(cp, "tp"), P(), P()),
        out_specs=P(cp, "tp"),
        check_vma=False,
    )
```

```python
import functools

import jax
import jax.numpy as jnp
from jax import lax
from jax.experimental import pallas as pl
from jax.experimental.pallas import tpu as pltpu
from jax.sharding import Mesh
from jax.sharding import PartitionSpec as P

HEAD_SIZE = 128
NEG = -1e30
SCALE2 = HEAD_SIZE ** (-0.5) * 1.4426950408889634
GROUP = 8
BLOCK = 512
PARTS = 4

bf16 = jnp.bfloat16
f32 = jnp.float32


def attend_kernel(places, n_arrays, has_fresh, first, last, rows, heads, *refs):
    info = refs[0]
    at = 1
    n_cached = len(places)
    arrays = refs[at : at + n_arrays]
    at += n_arrays
    q_ref = refs[at]
    at += 1
    if has_fresh:
        fresh_ref, fresh_mask = refs[at : at + 2]
        at += 2
    if not first:
        m_in, l_in, acc_in = refs[at : at + 3]
        at += 3
    if last:
        keep_ref, send_ref, lse_ref = refs[at : at + 3]
        at += 3
    else:
        m_ref, l_ref, acc_ref = refs[at : at + 3]
        at += 3
    kbuf, vbuf, qbuf, s_even, s_odd, p_even, p_odd, sems = refs[at : at + 8]
    at += 8
    if last:
        m_ref, l_ref, acc_ref = refs[at : at + 3]
    groups = heads // GROUP
    wide = GROUP * rows
    plen = info[0]

    def copies(i, slot):
        row = pl.multiple_of(slot * BLOCK, BLOCK)
        source, top = arrays[places[i][0]], places[i][1]
        return (
            pltpu.make_async_copy(
                source.at[pl.ds(top, BLOCK), :], kbuf.at[pl.ds(row, BLOCK), pl.ds(0, HEAD_SIZE)], sems.at[i]
            ),
            pltpu.make_async_copy(source.at[pl.ds(top + BLOCK, BLOCK), :], vbuf.at[pl.ds(row, BLOCK), :], sems.at[i]),
        )

    def visit(action):
        slot = jnp.int32(0)
        for i in range(n_cached):
            live = info[1 + i] < plen

            @pl.when(live)
            def _(slot=slot, i=i):
                action(i, slot)

            slot = slot + live.astype(jnp.int32)
        return slot

    def begin(i, slot):
        one, two = copies(i, slot)
        one.start()
        two.start()

    used = visit(begin)

    eye = (
        lax.broadcasted_iota(jnp.int32, (rows, HEAD_SIZE), 0) == lax.broadcasted_iota(jnp.int32, (rows, HEAD_SIZE), 1)
    ).astype(bf16)
    for h in range(heads):
        side, col = divmod(h, heads // 2)
        qbuf[pl.ds(h * rows, rows), 0:HEAD_SIZE] = q_ref[
            side * rows : (side + 1) * rows, col * HEAD_SIZE : (col + 1) * HEAD_SIZE
        ]
        qbuf[pl.ds(h * rows, rows), HEAD_SIZE : 2 * HEAD_SIZE] = eye

    def bias(i, slot):
        spot = lax.broadcasted_iota(jnp.int32, (BLOCK, HEAD_SIZE), 0) + info[1 + i]
        kbuf[pl.ds(pl.multiple_of(slot * BLOCK, BLOCK), BLOCK), pl.ds(HEAD_SIZE, HEAD_SIZE)] = jnp.where(
            spot < plen, 0.0, NEG
        ).astype(bf16)

    visit(bias)
    if has_fresh:
        sources, per = fresh_ref.shape[0], fresh_ref.shape[2]
        count = sources * per
        base = pl.multiple_of(used * BLOCK, BLOCK)
        kbuf[pl.ds(base, count), pl.ds(0, HEAD_SIZE)] = fresh_ref[:, 0].reshape(count, HEAD_SIZE)
        vbuf[pl.ds(base, count), :] = fresh_ref[:, 1].reshape(count, HEAD_SIZE)
        kbuf[pl.ds(base, count), pl.ds(HEAD_SIZE, HEAD_SIZE)] = fresh_mask[...]
        used = used + count // BLOCK

    if first:
        m_ref[...] = jnp.full_like(m_ref, NEG)
        l_ref[...] = jnp.zeros_like(l_ref)
        acc_ref[...] = jnp.zeros_like(acc_ref)
    else:
        m_ref[...] = m_in[...]
        l_ref[...] = l_in[...]
        acc_ref[...] = acc_in[...]

    def finish(i, slot):
        one, two = copies(i, slot)
        one.wait()
        two.wait()

    visit(finish)

    piece = wide // PARTS
    spans = [slice(j * piece, (j + 1) * piece) for j in range(PARTS)]

    def at_block(buf, b):
        return buf[pl.ds(pl.multiple_of(b * BLOCK, BLOCK), BLOCK), :]

    def qk(g, b, j):
        q = qbuf[pl.ds(pl.multiple_of(g * wide + j * piece, piece), piece), :]
        return lax.dot_general(at_block(kbuf, b), q, (((1,), (1,)), ((), ())), preferred_element_type=f32)

    def pv(b, p):
        return lax.dot_general(at_block(vbuf, b), p, (((0,), (0,)), ((), ())), preferred_element_type=f32)

    def after(g, b):
        end = b + 1 == used
        return jnp.where(end, g + 1, g), jnp.where(end, 0, b + 1)

    def turn(carry, s_now, p_now, s_next, p_before):
        g0, b0, old, g, b = carry
        gn, bn = after(g, b)
        factors = []
        for j, span in enumerate(spans):
            s_next[:, span] = qk(jnp.minimum(gn, groups - 1), bn, j)
            s = s_now[:, span]
            m = m_ref[g, :, span]
            new = jnp.maximum(m, jnp.max(s, axis=0, keepdims=True))
            factor = jnp.exp2((m - new) * SCALE2)
            p = jnp.exp2((s - new) * SCALE2)
            m_ref[g, :, span] = new
            l_ref[g, :, span] = l_ref[g, :, span] * factor + jnp.sum(p, axis=0, keepdims=True)
            p_now[:, span] = p.astype(bf16)
            acc_ref[g0, :, span] = acc_ref[g0, :, span] * old[j] + pv(b0, p_before[:, span])
            factors.append(factor)
        return g, b, tuple(factors), gn, bn

    zero = jnp.int32(0)
    p_odd[...] = jnp.zeros_like(p_odd)
    for j, span in enumerate(spans):
        s_even[:, span] = qk(zero, zero, j)

    def body(_, carry):
        carry = turn(carry, s_even, p_even, s_odd, p_odd)
        return turn(carry, s_odd, p_odd, s_even, p_even)

    ones = tuple(jnp.ones((1, piece), f32) for _ in range(PARTS))
    g0, b0, old, _, _ = lax.fori_loop(0, groups * used // 2, body, (zero, zero, ones, zero, zero))
    for j, span in enumerate(spans):
        acc_ref[g0, :, span] = acc_ref[g0, :, span] * old[j] + pv(b0, p_odd[:, span])

    if last:
        half = rows // 2
        for g in range(groups):
            total = l_ref[g]
            lse = m_ref[g] * SCALE2 + jnp.log2(total)
            out = (acc_ref[g] / total).T
            for j in range(GROUP):
                h = g * GROUP + j
                own = out[j * rows : (j + 1) * rows]
                keep_ref[:, h * HEAD_SIZE : (h + 1) * HEAD_SIZE] = own[:half]
                send_ref[:, h * HEAD_SIZE : (h + 1) * HEAD_SIZE] = own[half:].astype(bf16)
                lse_ref[h : h + 1, :] = lse[:, j * rows : (j + 1) * rows]


def attend(info, arrays, places, queries, heads, fresh=None, state=None, last=False):
    rows = queries.shape[0] // 2
    wide = GROUP * rows
    groups = heads // GROUP
    first = state is None
    n_cached = len(places)
    slots = n_cached + (0 if fresh is None else fresh[0].shape[0] * fresh[0].shape[2] // BLOCK)
    vm = pl.BlockSpec(memory_space=pltpu.VMEM)
    args = [info, *arrays, queries]
    specs = [pl.BlockSpec(memory_space=pltpu.SMEM)] + [pl.BlockSpec(memory_space=pl.ANY)] * len(arrays) + [vm]
    if fresh is not None:
        args += list(fresh)
        specs += [vm, vm]
    if not first:
        args += list(state)
        specs += [vm] * 3
    states = [
        ((groups, 1, wide), f32),
        ((groups, 1, wide), f32),
        ((groups, HEAD_SIZE, wide), f32),
    ]
    if last:
        outs = [
            jax.ShapeDtypeStruct((rows // 2, heads * HEAD_SIZE), f32),
            jax.ShapeDtypeStruct((rows // 2, heads * HEAD_SIZE), bf16),
            jax.ShapeDtypeStruct((heads, rows), f32),
        ]
    else:
        outs = [jax.ShapeDtypeStruct(s, d) for s, d in states]
    scratch = [
        pltpu.VMEM((slots * BLOCK, 2 * HEAD_SIZE), bf16),
        pltpu.VMEM((slots * BLOCK, HEAD_SIZE), bf16),
        pltpu.VMEM((heads * rows, 2 * HEAD_SIZE), bf16),
        pltpu.VMEM((BLOCK, wide), f32),
        pltpu.VMEM((BLOCK, wide), f32),
        pltpu.VMEM((BLOCK, wide), bf16),
        pltpu.VMEM((BLOCK, wide), bf16),
        pltpu.SemaphoreType.DMA((max(n_cached, 1),)),
    ]
    if last:
        scratch += [pltpu.VMEM(s, d) for s, d in states]
    return pl.pallas_call(
        functools.partial(attend_kernel, places, len(arrays), fresh is not None, first, last, rows, heads),
        out_shape=outs,
        in_specs=specs,
        out_specs=[vm] * 3,
        scratch_shapes=scratch,
        compiler_params=pltpu.CompilerParams(vmem_limit_bytes=24 * 2**20),
        cost_estimate=pl.CostEstimate(
            flops=4 * slots * BLOCK * heads * rows * HEAD_SIZE * 2,
            bytes_accessed=slots * BLOCK * HEAD_SIZE * 4,
            transcendentals=slots * BLOCK * heads * rows,
        ),
    )(*args)


def merge_kernel(heads, keep_ref, got_ref, mine_ref, theirs_ref, out_ref):
    half = keep_ref.shape[0]
    mine = mine_ref[...].T[:half]
    theirs = theirs_ref[...].T[half:]
    peak = jnp.maximum(mine, theirs)
    one = jnp.exp2(mine - peak)
    two = jnp.exp2(theirs - peak)
    total = one + two
    one = one / total
    two = two / total
    for h in range(heads):
        cols = slice(h * HEAD_SIZE, (h + 1) * HEAD_SIZE)
        out_ref[:, cols] = (
            keep_ref[:, cols] * one[:, h : h + 1] + got_ref[:, cols].astype(f32) * two[:, h : h + 1]
        ).astype(bf16)


def merge(heads, keep, got, mine, theirs):
    return pl.pallas_call(
        functools.partial(merge_kernel, heads),
        out_shape=jax.ShapeDtypeStruct(keep.shape, bf16),
        in_specs=[pl.BlockSpec(memory_space=pltpu.VMEM)] * 4,
        out_specs=pl.BlockSpec(memory_space=pltpu.VMEM),
        compiler_params=pltpu.CompilerParams(vmem_limit_bytes=8 * 2**20),
    )(keep, got, mine, theirs)


def step(query, fresh_key_rows, fresh_value_rows, cached_key_rows, cached_value_rows, prefix_len, stripe_owner):
    nx, nz, nc, ntp = (lax.axis_size(a) for a in ("x", "z", "c", "tp"))
    x, z, c = (lax.axis_index(a) for a in ("x", "z", "c"))
    parts = nx * nz * nc
    up = [(i, (i + 1) % nz) for i in range(nz)]
    down = [(i, (i - 1) % nz) for i in range(nz)]
    swap = [(0, 1), (1, 0)]

    own = jnp.concatenate([cached_key_rows, cached_value_rows], axis=0)
    other = lax.ppermute(own, "x", swap)

    both = jnp.concatenate([own, other], axis=0)

    def hop(above, below):
        return lax.ppermute(above, "z", up), lax.ppermute(below, "z", down)

    up1, down1 = hop(both, both)
    up2, down2 = hop(up1, down1)

    local = query.shape[0]
    width = query.shape[1] // ntp
    mixed = jnp.concatenate(
        [
            query.reshape(local, ntp, width),
            fresh_key_rows.reshape(local, ntp, HEAD_SIZE),
            fresh_value_rows.reshape(local, ntp, HEAD_SIZE),
        ],
        axis=2,
    ).reshape(local, ntp * (width + 2 * HEAD_SIZE))
    mixed = lax.all_to_all(mixed, "tp", split_axis=1, concat_axis=0, tiled=True)
    rows = mixed.shape[0]
    stripe = rows // parts
    heads = width // HEAD_SIZE
    order = jnp.arange(parts, dtype=jnp.int32)
    inverse = jnp.sum(jnp.where(stripe_owner[None, :] == order[:, None], order[None, :], 0), axis=1)
    half = width // 2
    chips = nx * nz
    per = rows // chips
    out_id = jnp.arange(2 * rows, dtype=jnp.int32)
    wanted = out_id // (2 * per) * per + out_id % per
    side = out_id // per % 2
    from_row = jnp.sum(jnp.where((wanted // stripe)[:, None] == order[None, :], inverse[None, :], 0), axis=1)
    from_row = from_row * stripe + wanted % stripe
    pick = (from_row[:, None] == jnp.arange(rows, dtype=jnp.int32)[None, :])
    left = (pick & (side == 0)[:, None]).astype(bf16)
    right = (pick & (side == 1)[:, None]).astype(bf16)
    arranged = jnp.dot(
        jnp.concatenate([left, right], axis=1),
        jnp.concatenate([mixed[:, :half], mixed[:, half:width]], axis=0),
        preferred_element_type=f32,
    ).astype(bf16)
    mine = lax.all_to_all(arranged, ("x", "z"), split_axis=0, concat_axis=0, tiled=True)
    peers = lax.ppermute(mine, "c", swap)

    def spot(side, rel, s, src, i):
        part = (src != c).astype(jnp.int32)
        owner = jnp.where(rel == 0, c, 1 - c)
        return part * 2 * rows + s * 2 * per + side * per + owner * stripe + i

    idx = jnp.arange(nc * rows, dtype=jnp.int32)
    i_, src_, s_, rel_ = idx % stripe, idx // stripe % nc, idx // (stripe * nc) % chips, idx // rows
    wide_id = jnp.arange(2 * nc * rows, dtype=jnp.int32)
    low = wide_id % (nc * rows)
    where = spot(wide_id // (nc * rows), low // rows, low // (stripe * nc) % chips, low // stripe % nc, low % stripe)
    choose = (where[:, None] == wide_id[None, :]).astype(bf16)
    queries = jnp.dot(choose, jnp.concatenate([mine, peers], axis=0), preferred_element_type=f32).astype(bf16)
    owner_ = (x * nz + z) * nc + jnp.where(rel_ == 0, c, 1 - c)
    residue_ = jnp.sum(jnp.where(owner_[:, None] == order[None, :], inverse[None, :], 0), axis=1)
    natural = (s_ * nc + src_) * rows + residue_ * stripe + i_

    fresh = jnp.concatenate(
        [mixed[:, width : width + HEAD_SIZE], mixed[:, width + HEAD_SIZE :]], axis=0
    ).reshape(1, 2, rows, HEAD_SIZE)
    key_id = jnp.arange(nx * nz * rows, dtype=jnp.int32)
    key_natural = (key_id // rows * nc + c) * rows + key_id % rows
    fresh_mask = jnp.where(key_natural[:, None] <= natural[None, :], 0.0, NEG).astype(bf16)

    slots = cached_key_rows.shape[0]

    def info_of(where):
        flip = jnp.array([w[0] for w in where], jnp.int32)
        step = jnp.array([w[1] + nz for w in where], jnp.int32)
        starts = ((jnp.where(flip == 0, x, 1 - x) * nz + (z + step) % nz) * nc + c) * slots
        return jnp.concatenate([prefix_len, starts.astype(jnp.int32)])

    def around(step):
        return [(0, -step), (1, -step), (0, step), (1, step)]

    two = 2 * slots
    near = ((0, 0), (0, two), (1, 0), (1, two), (2, 0), (2, two))
    pair = ((0, 0), (0, two), (1, 0), (1, two))
    first_info = info_of([(0, 0), (1, 0)] + around(1))
    state = attend(first_info, [both, up1, down1], near, queries, heads)
    up2, down2, state = lax.optimization_barrier((up2, down2, state))
    up3, down3 = hop(up2, down2)
    state = attend(info_of(around(2)), [up2, down2], pair, queries, heads, state=state)
    up3, down3, fresh, state = lax.optimization_barrier((up3, down3, fresh, state))
    up4 = lax.ppermute(up3[:two], "z", up)
    down4 = lax.ppermute(down3[two:], "z", down)
    fresh = jnp.broadcast_to(fresh, (chips, 2, rows, HEAD_SIZE))
    fresh = lax.all_to_all(fresh, ("x", "z"), split_axis=0, concat_axis=0, tiled=True)
    state = attend(info_of(around(3)), [up3, down3], pair, queries, heads, state=state)
    keep, give, lse = attend(
        info_of([(0, 4), (1, 4)]),
        [up4, down4],
        ((0, 0), (1, 0)),
        queries,
        heads,
        fresh=(fresh, fresh_mask),
        state=state,
        last=True,
    )
    got = lax.ppermute(give, "c", swap)
    their_lse = lax.ppermute(lse, "c", swap)
    return merge(heads, keep, got, lse, their_lse)


def solution(mesh):
    devices = mesh.devices
    parts = Mesh(devices.reshape(2, devices.shape[0] // 4, 2, devices.shape[1]), ("x", "z", "c", "tp"))
    rows = ("x", "z", "c", "tp")
    cp = ("x", "z", "c")
    return jax.shard_map(
        step,
        mesh=parts,
        in_specs=(P(rows, None), P(rows, None), P(rows, None), P(cp, "tp"), P(cp, "tp"), P(), P()),
        out_specs=P(cp, "tp"),
        check_vma=False,
    )
```

```python
import functools

import jax
import jax.numpy as jnp
from jax import lax
from jax.experimental import pallas as pl
from jax.experimental.pallas import tpu as pltpu
from jax.sharding import Mesh
from jax.sharding import PartitionSpec as P

HEAD_SIZE = 128
NEG = -1e30
SCALE2 = HEAD_SIZE ** (-0.5) * 1.4426950408889634
GROUP = 8
BLOCK = 512
PARTS = 4

bf16 = jnp.bfloat16
f32 = jnp.float32


def attend_kernel(places, n_arrays, has_fresh, first, last, rows, heads, *refs):
    info = refs[0]
    at = 1
    n_cached = len(places)
    arrays = refs[at : at + n_arrays]
    at += n_arrays
    q_ref = refs[at]
    at += 1
    if has_fresh:
        fresh_ref, fresh_mask = refs[at : at + 2]
        at += 2
    if not first:
        m_in, l_in, acc_in = refs[at : at + 3]
        at += 3
    if last:
        keep_ref, send_ref, lse_ref = refs[at : at + 3]
        at += 3
    else:
        m_ref, l_ref, acc_out = refs[at : at + 3]
        at += 3
    kbuf, vbuf, qbuf, s_even, s_odd, p_even, p_odd, sems = refs[at : at + 8]
    at += 8
    acc_ref = refs[at]
    at += 1
    if last:
        m_ref, l_ref = refs[at : at + 2]
    groups = heads // GROUP
    wide = GROUP * rows
    plen = info[0]

    def copies(i, slot):
        row = pl.multiple_of(slot * BLOCK, BLOCK)
        source, top = arrays[places[i][0]], places[i][1]
        return (
            pltpu.make_async_copy(
                source.at[pl.ds(top, BLOCK), :], kbuf.at[pl.ds(row, BLOCK), pl.ds(0, HEAD_SIZE)], sems.at[i]
            ),
            pltpu.make_async_copy(source.at[pl.ds(top + BLOCK, BLOCK), :], vbuf.at[pl.ds(row, BLOCK), :], sems.at[i]),
        )

    def visit(action):
        slot = jnp.int32(0)
        for i in range(n_cached):
            live = info[1 + i] < plen

            @pl.when(live)
            def _(slot=slot, i=i):
                action(i, slot)

            slot = slot + live.astype(jnp.int32)
        return slot

    def begin(i, slot):
        one, two = copies(i, slot)
        one.start()
        two.start()

    used = visit(begin)
    if not first:
        fetch = pltpu.make_async_copy(acc_in, acc_ref, sems.at[n_cached])
        fetch.start()

    eye = (
        lax.broadcasted_iota(jnp.int32, (rows, HEAD_SIZE), 0) == lax.broadcasted_iota(jnp.int32, (rows, HEAD_SIZE), 1)
    ).astype(bf16)
    for h in range(heads):
        side, col = divmod(h, heads // 2)
        qbuf[pl.ds(h * rows, rows), 0:HEAD_SIZE] = q_ref[
            side * rows : (side + 1) * rows, col * HEAD_SIZE : (col + 1) * HEAD_SIZE
        ]
        qbuf[pl.ds(h * rows, rows), HEAD_SIZE : 2 * HEAD_SIZE] = eye

    def bias(i, slot):
        spot = lax.broadcasted_iota(jnp.int32, (BLOCK, HEAD_SIZE), 0) + info[1 + i]
        kbuf[pl.ds(pl.multiple_of(slot * BLOCK, BLOCK), BLOCK), pl.ds(HEAD_SIZE, HEAD_SIZE)] = jnp.where(
            spot < plen, 0.0, NEG
        ).astype(bf16)

    visit(bias)
    if has_fresh:
        sources, per = fresh_ref.shape[0], fresh_ref.shape[2]
        count = sources * per
        base = pl.multiple_of(used * BLOCK, BLOCK)
        kbuf[pl.ds(base, count), pl.ds(0, HEAD_SIZE)] = fresh_ref[:, 0].reshape(count, HEAD_SIZE)
        vbuf[pl.ds(base, count), :] = fresh_ref[:, 1].reshape(count, HEAD_SIZE)
        kbuf[pl.ds(base, count), pl.ds(HEAD_SIZE, HEAD_SIZE)] = fresh_mask[...]
        used = used + count // BLOCK

    if first:
        m_ref[...] = jnp.full_like(m_ref, NEG)
        l_ref[...] = jnp.zeros_like(l_ref)
        acc_ref[...] = jnp.zeros_like(acc_ref)
    else:
        m_ref[...] = m_in[...]
        l_ref[...] = l_in[...]
        fetch.wait()

    def finish(i, slot):
        one, two = copies(i, slot)
        one.wait()
        two.wait()

    visit(finish)

    piece = wide // PARTS
    spans = [slice(j * piece, (j + 1) * piece) for j in range(PARTS)]

    def at_block(buf, b):
        return buf[pl.ds(pl.multiple_of(b * BLOCK, BLOCK), BLOCK), :]

    def qk(g, b, j):
        q = qbuf[pl.ds(pl.multiple_of(g * wide + j * piece, piece), piece), :]
        return lax.dot_general(at_block(kbuf, b), q, (((1,), (1,)), ((), ())), preferred_element_type=f32)

    def pv(b, p):
        return lax.dot_general(at_block(vbuf, b), p, (((0,), (0,)), ((), ())), preferred_element_type=f32)

    def after(g, b):
        end = b + 1 == used
        return jnp.where(end, g + 1, g), jnp.where(end, 0, b + 1)

    def turn(carry, s_now, p_now, s_next, p_before):
        g0, b0, old, g, b = carry
        gn, bn = after(g, b)
        factors = []
        for j, span in enumerate(spans):
            s_next[:, span] = qk(jnp.minimum(gn, groups - 1), bn, j)
            s = s_now[:, span]
            m = m_ref[g, :, span]
            new = jnp.maximum(m, jnp.max(s, axis=0, keepdims=True))
            factor = jnp.exp2((m - new) * SCALE2)
            p = jnp.exp2((s - new) * SCALE2)
            m_ref[g, :, span] = new
            l_ref[g, :, span] = l_ref[g, :, span] * factor + jnp.sum(p, axis=0, keepdims=True)
            p_now[:, span] = p.astype(bf16)
            acc_ref[g0, :, span] = acc_ref[g0, :, span] * old[j] + pv(b0, p_before[:, span])
            factors.append(factor)
        return g, b, tuple(factors), gn, bn

    zero = jnp.int32(0)
    p_odd[...] = jnp.zeros_like(p_odd)
    for j, span in enumerate(spans):
        s_even[:, span] = qk(zero, zero, j)

    def body(_, carry):
        carry = turn(carry, s_even, p_even, s_odd, p_odd)
        return turn(carry, s_odd, p_odd, s_even, p_even)

    ones = tuple(jnp.ones((1, piece), f32) for _ in range(PARTS))
    g0, b0, old, _, _ = lax.fori_loop(0, groups * used // 2, body, (zero, zero, ones, zero, zero))
    for j, span in enumerate(spans):
        acc_ref[g0, :, span] = acc_ref[g0, :, span] * old[j] + pv(b0, p_odd[:, span])

    if not last:
        store = pltpu.make_async_copy(acc_ref, acc_out, sems.at[n_cached])
        store.start()
        store.wait()
    if last:
        half = rows // 2
        for g in range(groups):
            total = l_ref[g]
            lse = m_ref[g] * SCALE2 + jnp.log2(total)
            out = (acc_ref[g] / total).T
            for j in range(GROUP):
                h = g * GROUP + j
                own = out[j * rows : (j + 1) * rows]
                keep_ref[:, h * HEAD_SIZE : (h + 1) * HEAD_SIZE] = own[:half]
                send_ref[:, h * HEAD_SIZE : (h + 1) * HEAD_SIZE] = own[half:].astype(bf16)
                lse_ref[h : h + 1, :] = lse[:, j * rows : (j + 1) * rows]


def attend(info, arrays, places, queries, heads, fresh=None, state=None, last=False):
    rows = queries.shape[0] // 2
    wide = GROUP * rows
    groups = heads // GROUP
    first = state is None
    n_cached = len(places)
    slots = n_cached + (0 if fresh is None else fresh[0].shape[0] * fresh[0].shape[2] // BLOCK)
    vm = pl.BlockSpec(memory_space=pltpu.VMEM)
    args = [info, *arrays, queries]
    specs = [pl.BlockSpec(memory_space=pltpu.SMEM)] + [pl.BlockSpec(memory_space=pl.ANY)] * len(arrays) + [vm]
    if fresh is not None:
        args += list(fresh)
        specs += [vm, vm]
    if not first:
        args += list(state)
        specs += [vm, vm, pl.BlockSpec(memory_space=pl.ANY)]
    states = [
        ((groups, 1, wide), f32),
        ((groups, 1, wide), f32),
        ((groups, HEAD_SIZE, wide), f32),
    ]
    if last:
        outs = [
            jax.ShapeDtypeStruct((rows // 2, heads * HEAD_SIZE), f32),
            jax.ShapeDtypeStruct((rows // 2, heads * HEAD_SIZE), bf16),
            jax.ShapeDtypeStruct((heads, rows), f32),
        ]
    else:
        outs = [jax.ShapeDtypeStruct(s, d) for s, d in states]
    scratch = [
        pltpu.VMEM((slots * BLOCK, 2 * HEAD_SIZE), bf16),
        pltpu.VMEM((slots * BLOCK, HEAD_SIZE), bf16),
        pltpu.VMEM((heads * rows, 2 * HEAD_SIZE), bf16),
        pltpu.VMEM((BLOCK, wide), f32),
        pltpu.VMEM((BLOCK, wide), f32),
        pltpu.VMEM((BLOCK, wide), bf16),
        pltpu.VMEM((BLOCK, wide), bf16),
        pltpu.SemaphoreType.DMA((n_cached + 1,)),
        pltpu.VMEM(*states[2]),
    ]
    if last:
        scratch += [pltpu.VMEM(s, d) for s, d in states[:2]]
    return pl.pallas_call(
        functools.partial(attend_kernel, places, len(arrays), fresh is not None, first, last, rows, heads),
        out_shape=outs,
        in_specs=specs,
        out_specs=[vm, vm, vm if last else pl.BlockSpec(memory_space=pl.ANY)],
        scratch_shapes=scratch,
        compiler_params=pltpu.CompilerParams(vmem_limit_bytes=24 * 2**20),
        cost_estimate=pl.CostEstimate(
            flops=4 * slots * BLOCK * heads * rows * HEAD_SIZE * 2,
            bytes_accessed=slots * BLOCK * HEAD_SIZE * 4,
            transcendentals=slots * BLOCK * heads * rows,
        ),
    )(*args)


def merge_kernel(heads, keep_ref, got_ref, mine_ref, theirs_ref, out_ref):
    half = keep_ref.shape[0]
    mine = mine_ref[...].T[:half]
    theirs = theirs_ref[...].T[half:]
    peak = jnp.maximum(mine, theirs)
    one = jnp.exp2(mine - peak)
    two = jnp.exp2(theirs - peak)
    total = one + two
    one = one / total
    two = two / total
    for h in range(heads):
        cols = slice(h * HEAD_SIZE, (h + 1) * HEAD_SIZE)
        out_ref[:, cols] = (
            keep_ref[:, cols] * one[:, h : h + 1] + got_ref[:, cols].astype(f32) * two[:, h : h + 1]
        ).astype(bf16)


def merge(heads, keep, got, mine, theirs):
    return pl.pallas_call(
        functools.partial(merge_kernel, heads),
        out_shape=jax.ShapeDtypeStruct(keep.shape, bf16),
        in_specs=[pl.BlockSpec(memory_space=pltpu.VMEM)] * 4,
        out_specs=pl.BlockSpec(memory_space=pltpu.VMEM),
        compiler_params=pltpu.CompilerParams(vmem_limit_bytes=8 * 2**20),
    )(keep, got, mine, theirs)


def step(query, fresh_key_rows, fresh_value_rows, cached_key_rows, cached_value_rows, prefix_len, stripe_owner):
    nx, nz, nc, ntp = (lax.axis_size(a) for a in ("x", "z", "c", "tp"))
    x, z, c = (lax.axis_index(a) for a in ("x", "z", "c"))
    parts = nx * nz * nc
    up = [(i, (i + 1) % nz) for i in range(nz)]
    down = [(i, (i - 1) % nz) for i in range(nz)]
    swap = [(0, 1), (1, 0)]

    own = jnp.concatenate([cached_key_rows, cached_value_rows], axis=0)
    other = lax.ppermute(own, "x", swap)

    both = jnp.concatenate([own, other], axis=0)

    def hop(above, below):
        return lax.ppermute(above, "z", up), lax.ppermute(below, "z", down)

    up1, down1 = hop(both, both)
    up2, down2 = hop(up1, down1)

    local = query.shape[0]
    width = query.shape[1] // ntp
    mixed = jnp.concatenate(
        [
            query.reshape(local, ntp, width),
            fresh_key_rows.reshape(local, ntp, HEAD_SIZE),
            fresh_value_rows.reshape(local, ntp, HEAD_SIZE),
        ],
        axis=2,
    ).reshape(local, ntp * (width + 2 * HEAD_SIZE))
    mixed = lax.all_to_all(mixed, "tp", split_axis=1, concat_axis=0, tiled=True)
    rows = mixed.shape[0]
    stripe = rows // parts
    heads = width // HEAD_SIZE
    order = jnp.arange(parts, dtype=jnp.int32)
    inverse = jnp.sum(jnp.where(stripe_owner[None, :] == order[:, None], order[None, :], 0), axis=1)
    half = width // 2
    chips = nx * nz
    per = rows // chips
    out_id = jnp.arange(2 * rows, dtype=jnp.int32)
    wanted = out_id // (2 * per) * per + out_id % per
    side = out_id // per % 2
    from_row = jnp.sum(jnp.where((wanted // stripe)[:, None] == order[None, :], inverse[None, :], 0), axis=1)
    from_row = from_row * stripe + wanted % stripe
    pick = (from_row[:, None] == jnp.arange(rows, dtype=jnp.int32)[None, :])
    left = (pick & (side == 0)[:, None]).astype(bf16)
    right = (pick & (side == 1)[:, None]).astype(bf16)
    arranged = jnp.dot(
        jnp.concatenate([left, right], axis=1),
        jnp.concatenate([mixed[:, :half], mixed[:, half:width]], axis=0),
        preferred_element_type=f32,
    ).astype(bf16)
    mine = lax.all_to_all(arranged, ("x", "z"), split_axis=0, concat_axis=0, tiled=True)
    peers = lax.ppermute(mine, "c", swap)

    def spot(side, rel, s, src, i):
        part = (src != c).astype(jnp.int32)
        owner = jnp.where(rel == 0, c, 1 - c)
        return part * 2 * rows + s * 2 * per + side * per + owner * stripe + i

    idx = jnp.arange(nc * rows, dtype=jnp.int32)
    i_, src_, s_, rel_ = idx % stripe, idx // stripe % nc, idx // (stripe * nc) % chips, idx // rows
    wide_id = jnp.arange(2 * nc * rows, dtype=jnp.int32)
    low = wide_id % (nc * rows)
    where = spot(wide_id // (nc * rows), low // rows, low // (stripe * nc) % chips, low // stripe % nc, low % stripe)
    choose = (where[:, None] == wide_id[None, :]).astype(bf16)
    queries = jnp.dot(choose, jnp.concatenate([mine, peers], axis=0), preferred_element_type=f32).astype(bf16)
    owner_ = (x * nz + z) * nc + jnp.where(rel_ == 0, c, 1 - c)
    residue_ = jnp.sum(jnp.where(owner_[:, None] == order[None, :], inverse[None, :], 0), axis=1)
    natural = (s_ * nc + src_) * rows + residue_ * stripe + i_

    fresh = jnp.concatenate(
        [mixed[:, width : width + HEAD_SIZE], mixed[:, width + HEAD_SIZE :]], axis=0
    ).reshape(1, 2, rows, HEAD_SIZE)
    key_id = jnp.arange(nx * nz * rows, dtype=jnp.int32)
    key_natural = (key_id // rows * nc + c) * rows + key_id % rows
    fresh_mask = jnp.where(key_natural[:, None] <= natural[None, :], 0.0, NEG).astype(bf16)

    slots = cached_key_rows.shape[0]

    def info_of(where):
        flip = jnp.array([w[0] for w in where], jnp.int32)
        step = jnp.array([w[1] + nz for w in where], jnp.int32)
        starts = ((jnp.where(flip == 0, x, 1 - x) * nz + (z + step) % nz) * nc + c) * slots
        return jnp.concatenate([prefix_len, starts.astype(jnp.int32)])

    def around(step):
        return [(0, -step), (1, -step), (0, step), (1, step)]

    two = 2 * slots
    near = ((0, 0), (0, two), (1, 0), (1, two), (2, 0), (2, two))
    pair = ((0, 0), (0, two), (1, 0), (1, two))
    first_info = info_of([(0, 0), (1, 0)] + around(1))
    state = attend(first_info, [both, up1, down1], near, queries, heads)
    up2, down2, state = lax.optimization_barrier((up2, down2, state))
    up3, down3 = hop(up2, down2)
    second_info = info_of(around(2))
    state = attend(second_info, [up2, down2], pair, queries, heads, state=state)
    fresh, state = lax.optimization_barrier((fresh, state))
    up4 = lax.ppermute(up3[:two], "z", up)
    down4 = lax.ppermute(down3[two:], "z", down)
    fresh = jnp.broadcast_to(fresh, (chips, 2, rows, HEAD_SIZE))
    fresh = lax.all_to_all(fresh, ("x", "z"), split_axis=0, concat_axis=0, tiled=True)
    third_info = info_of(around(3))
    state = attend(third_info, [up3, down3], pair, queries, heads, state=state)
    keep, give, lse = attend(
        info_of([(0, 4), (1, 4)]),
        [up4, down4],
        ((0, 0), (1, 0)),
        queries,
        heads,
        fresh=(fresh, fresh_mask),
        state=state,
        last=True,
    )
    got = lax.ppermute(give, "c", swap)
    their_lse = lax.ppermute(lse, "c", swap)
    return merge(heads, keep, got, lse, their_lse)


def solution(mesh):
    devices = mesh.devices
    parts = Mesh(devices.reshape(2, devices.shape[0] // 4, 2, devices.shape[1]), ("x", "z", "c", "tp"))
    rows = ("x", "z", "c", "tp")
    cp = ("x", "z", "c")
    return jax.shard_map(
        step,
        mesh=parts,
        in_specs=(P(rows, None), P(rows, None), P(rows, None), P(cp, "tp"), P(cp, "tp"), P(), P()),
        out_specs=P(cp, "tp"),
        check_vma=False,
    )
```

```python
import functools

import jax
import jax.numpy as jnp
from jax import lax
from jax.experimental import pallas as pl
from jax.experimental.pallas import tpu as pltpu
from jax.sharding import Mesh
from jax.sharding import PartitionSpec as P

HEAD_SIZE = 128
NEG = -1e30
SCALE2 = HEAD_SIZE ** (-0.5) * 1.4426950408889634
GROUP = 8
BLOCK = 512
PARTS = 4

bf16 = jnp.bfloat16
f32 = jnp.float32


def attend_kernel(places, n_arrays, has_fresh, first, last, rows, heads, *refs):
    info = refs[0]
    at = 1
    n_cached = len(places)
    arrays = refs[at : at + n_arrays]
    at += n_arrays
    q_ref = refs[at]
    at += 1
    if has_fresh:
        fresh_refs, fresh_mask = refs[at : at + 2], refs[at + 2]
        at += 3
    if not first:
        m_in, l_in, acc_in = refs[at : at + 3]
        at += 3
    if last:
        keep_ref, send_ref, lse_ref = refs[at : at + 3]
        at += 3
    else:
        m_ref, l_ref, acc_out = refs[at : at + 3]
        at += 3
    kbuf, vbuf, qbuf, s_even, s_odd, p_even, p_odd, sems = refs[at : at + 8]
    at += 8
    acc_ref = refs[at]
    at += 1
    if last:
        m_ref, l_ref = refs[at : at + 2]
    groups = heads // GROUP
    wide = GROUP * rows
    plen = info[0]

    def copies(i, slot):
        row = pl.multiple_of(slot * BLOCK, BLOCK)
        source, top = arrays[places[i][0]], places[i][1]
        return (
            pltpu.make_async_copy(
                source.at[pl.ds(top, BLOCK), :], kbuf.at[pl.ds(row, BLOCK), pl.ds(0, HEAD_SIZE)], sems.at[i]
            ),
            pltpu.make_async_copy(source.at[pl.ds(top + BLOCK, BLOCK), :], vbuf.at[pl.ds(row, BLOCK), :], sems.at[i]),
        )

    def visit(action):
        slot = jnp.int32(0)
        for i in range(n_cached):
            live = info[1 + i] < plen

            @pl.when(live)
            def _(slot=slot, i=i):
                action(i, slot)

            slot = slot + live.astype(jnp.int32)
        return slot

    def begin(i, slot):
        one, two = copies(i, slot)
        one.start()
        two.start()

    used = visit(begin)
    if not first:
        fetch = pltpu.make_async_copy(acc_in, acc_ref, sems.at[n_cached])
        fetch.start()

    eye = (
        lax.broadcasted_iota(jnp.int32, (rows, HEAD_SIZE), 0) == lax.broadcasted_iota(jnp.int32, (rows, HEAD_SIZE), 1)
    ).astype(bf16)
    for h in range(heads):
        side, col = divmod(h, heads // 2)
        qbuf[pl.ds(h * rows, rows), 0:HEAD_SIZE] = q_ref[
            side * rows : (side + 1) * rows, col * HEAD_SIZE : (col + 1) * HEAD_SIZE
        ]
        qbuf[pl.ds(h * rows, rows), HEAD_SIZE : 2 * HEAD_SIZE] = eye

    def bias(i, slot):
        spot = lax.broadcasted_iota(jnp.int32, (BLOCK, HEAD_SIZE), 0) + info[1 + i]
        kbuf[pl.ds(pl.multiple_of(slot * BLOCK, BLOCK), BLOCK), pl.ds(HEAD_SIZE, HEAD_SIZE)] = jnp.where(
            spot < plen, 0.0, NEG
        ).astype(bf16)

    visit(bias)
    if has_fresh:
        sources, _, per, _ = fresh_refs[0].shape
        count = sources * per
        for n, ref in enumerate(fresh_refs):
            base = pl.multiple_of((used + n * count // BLOCK) * BLOCK, BLOCK)
            kbuf[pl.ds(base, count), pl.ds(0, HEAD_SIZE)] = ref[:, 0].reshape(count, HEAD_SIZE)
            vbuf[pl.ds(base, count), :] = ref[:, 1].reshape(count, HEAD_SIZE)
            kbuf[pl.ds(base, count), pl.ds(HEAD_SIZE, HEAD_SIZE)] = fresh_mask[n * count : (n + 1) * count]
        used = used + 2 * count // BLOCK

    if first:
        m_ref[...] = jnp.full_like(m_ref, NEG)
        l_ref[...] = jnp.zeros_like(l_ref)
        acc_ref[...] = jnp.zeros_like(acc_ref)
    else:
        m_ref[...] = m_in[...]
        l_ref[...] = l_in[...]
        fetch.wait()

    def finish(i, slot):
        one, two = copies(i, slot)
        one.wait()
        two.wait()

    visit(finish)

    piece = wide // PARTS
    spans = [slice(j * piece, (j + 1) * piece) for j in range(PARTS)]

    def at_block(buf, b):
        return buf[pl.ds(pl.multiple_of(b * BLOCK, BLOCK), BLOCK), :]

    def qk(g, b, j):
        q = qbuf[pl.ds(pl.multiple_of(g * wide + j * piece, piece), piece), :]
        return lax.dot_general(at_block(kbuf, b), q, (((1,), (1,)), ((), ())), preferred_element_type=f32)

    def pv(b, p):
        return lax.dot_general(at_block(vbuf, b), p, (((0,), (0,)), ((), ())), preferred_element_type=f32)

    def after(g, b):
        end = b + 1 == used
        return jnp.where(end, g + 1, g), jnp.where(end, 0, b + 1)

    def turn(carry, s_now, p_now, s_next, p_before):
        g0, b0, old, g, b = carry
        gn, bn = after(g, b)
        factors = []
        for j, span in enumerate(spans):
            s_next[:, span] = qk(jnp.minimum(gn, groups - 1), bn, j)
            s = s_now[:, span]
            m = m_ref[g, :, span]
            new = jnp.maximum(m, jnp.max(s, axis=0, keepdims=True))
            factor = jnp.exp2((m - new) * SCALE2)
            p = jnp.exp2((s - new) * SCALE2)
            m_ref[g, :, span] = new
            l_ref[g, :, span] = l_ref[g, :, span] * factor + jnp.sum(p, axis=0, keepdims=True)
            p_now[:, span] = p.astype(bf16)
            acc_ref[g0, :, span] = acc_ref[g0, :, span] * old[j] + pv(b0, p_before[:, span])
            factors.append(factor)
        return g, b, tuple(factors), gn, bn

    zero = jnp.int32(0)
    p_odd[...] = jnp.zeros_like(p_odd)
    for j, span in enumerate(spans):
        s_even[:, span] = qk(zero, zero, j)

    def body(_, carry):
        carry = turn(carry, s_even, p_even, s_odd, p_odd)
        return turn(carry, s_odd, p_odd, s_even, p_even)

    ones = tuple(jnp.ones((1, piece), f32) for _ in range(PARTS))
    g0, b0, old, _, _ = lax.fori_loop(0, groups * used // 2, body, (zero, zero, ones, zero, zero))
    for j, span in enumerate(spans):
        acc_ref[g0, :, span] = acc_ref[g0, :, span] * old[j] + pv(b0, p_odd[:, span])

    if not last:
        store = pltpu.make_async_copy(acc_ref, acc_out, sems.at[n_cached])
        store.start()
        store.wait()
    if last:
        half = rows // 2
        for g in range(groups):
            total = l_ref[g]
            lse = m_ref[g] * SCALE2 + jnp.log2(total)
            out = (acc_ref[g] / total).T
            for j in range(GROUP):
                h = g * GROUP + j
                own = out[j * rows : (j + 1) * rows]
                keep_ref[:, h * HEAD_SIZE : (h + 1) * HEAD_SIZE] = own[:half]
                send_ref[:, h * HEAD_SIZE : (h + 1) * HEAD_SIZE] = own[half:].astype(bf16)
                lse_ref[h : h + 1, :] = lse[:, j * rows : (j + 1) * rows]


def attend(info, arrays, places, queries, heads, fresh=None, state=None, last=False):
    rows = queries.shape[0] // 2
    wide = GROUP * rows
    groups = heads // GROUP
    first = state is None
    n_cached = len(places)
    slots = n_cached + (0 if fresh is None else 2 * fresh[0].shape[0] * fresh[0].shape[2] // BLOCK)
    vm = pl.BlockSpec(memory_space=pltpu.VMEM)
    args = [info, *arrays, queries]
    specs = [pl.BlockSpec(memory_space=pltpu.SMEM)] + [pl.BlockSpec(memory_space=pl.ANY)] * len(arrays) + [vm]
    if fresh is not None:
        args += list(fresh)
        specs += [vm, vm, vm]
    if not first:
        args += list(state)
        specs += [vm, vm, pl.BlockSpec(memory_space=pl.ANY)]
    states = [
        ((groups, 1, wide), f32),
        ((groups, 1, wide), f32),
        ((groups, HEAD_SIZE, wide), f32),
    ]
    if last:
        outs = [
            jax.ShapeDtypeStruct((rows // 2, heads * HEAD_SIZE), f32),
            jax.ShapeDtypeStruct((rows // 2, heads * HEAD_SIZE), bf16),
            jax.ShapeDtypeStruct((heads, rows), f32),
        ]
    else:
        outs = [jax.ShapeDtypeStruct(s, d) for s, d in states]
    scratch = [
        pltpu.VMEM((slots * BLOCK, 2 * HEAD_SIZE), bf16),
        pltpu.VMEM((slots * BLOCK, HEAD_SIZE), bf16),
        pltpu.VMEM((heads * rows, 2 * HEAD_SIZE), bf16),
        pltpu.VMEM((BLOCK, wide), f32),
        pltpu.VMEM((BLOCK, wide), f32),
        pltpu.VMEM((BLOCK, wide), bf16),
        pltpu.VMEM((BLOCK, wide), bf16),
        pltpu.SemaphoreType.DMA((n_cached + 1,)),
        pltpu.VMEM(*states[2]),
    ]
    if last:
        scratch += [pltpu.VMEM(s, d) for s, d in states[:2]]
    return pl.pallas_call(
        functools.partial(attend_kernel, places, len(arrays), fresh is not None, first, last, rows, heads),
        out_shape=outs,
        in_specs=specs,
        out_specs=[vm, vm, vm if last else pl.BlockSpec(memory_space=pl.ANY)],
        scratch_shapes=scratch,
        compiler_params=pltpu.CompilerParams(vmem_limit_bytes=24 * 2**20),
        cost_estimate=pl.CostEstimate(
            flops=4 * slots * BLOCK * heads * rows * HEAD_SIZE * 2,
            bytes_accessed=slots * BLOCK * HEAD_SIZE * 4,
            transcendentals=slots * BLOCK * heads * rows,
        ),
    )(*args)


def merge_kernel(heads, keep_ref, got_ref, mine_ref, theirs_ref, out_ref):
    half = keep_ref.shape[0]
    mine = mine_ref[...].T[:half]
    theirs = theirs_ref[...].T[half:]
    peak = jnp.maximum(mine, theirs)
    one = jnp.exp2(mine - peak)
    two = jnp.exp2(theirs - peak)
    total = one + two
    one = one / total
    two = two / total
    for h in range(heads):
        cols = slice(h * HEAD_SIZE, (h + 1) * HEAD_SIZE)
        out_ref[:, cols] = (
            keep_ref[:, cols] * one[:, h : h + 1] + got_ref[:, cols].astype(f32) * two[:, h : h + 1]
        ).astype(bf16)


def merge(heads, keep, got, mine, theirs):
    return pl.pallas_call(
        functools.partial(merge_kernel, heads),
        out_shape=jax.ShapeDtypeStruct(keep.shape, bf16),
        in_specs=[pl.BlockSpec(memory_space=pltpu.VMEM)] * 4,
        out_specs=pl.BlockSpec(memory_space=pltpu.VMEM),
        compiler_params=pltpu.CompilerParams(vmem_limit_bytes=8 * 2**20),
    )(keep, got, mine, theirs)


def step(query, fresh_key_rows, fresh_value_rows, cached_key_rows, cached_value_rows, prefix_len, stripe_owner):
    nx, nz, nc, ntp = (lax.axis_size(a) for a in ("x", "z", "c", "tp"))
    x, z, c = (lax.axis_index(a) for a in ("x", "z", "c"))
    parts = nx * nz * nc
    up = [(i, (i + 1) % nz) for i in range(nz)]
    down = [(i, (i - 1) % nz) for i in range(nz)]
    swap = [(0, 1), (1, 0)]

    own = jnp.concatenate([cached_key_rows, cached_value_rows], axis=0)
    other = lax.ppermute(own, "x", swap)

    both = jnp.concatenate([own, other], axis=0)

    def hop(above, below):
        return lax.ppermute(above, "z", up), lax.ppermute(below, "z", down)

    up1, down1 = hop(both, both)
    up2, down2 = hop(up1, down1)

    local = query.shape[0]
    width = query.shape[1] // ntp
    mixed = jnp.concatenate(
        [
            query.reshape(local, ntp, width),
            fresh_key_rows.reshape(local, ntp, HEAD_SIZE),
            fresh_value_rows.reshape(local, ntp, HEAD_SIZE),
        ],
        axis=2,
    ).reshape(local, ntp * (width + 2 * HEAD_SIZE))
    mixed = lax.all_to_all(mixed, "tp", split_axis=1, concat_axis=0, tiled=True)
    rows = mixed.shape[0]
    stripe = rows // parts
    heads = width // HEAD_SIZE
    order = jnp.arange(parts, dtype=jnp.int32)
    inverse = jnp.sum(jnp.where(stripe_owner[None, :] == order[:, None], order[None, :], 0), axis=1)
    half = width // 2
    chips = nx * nz
    per = rows // chips
    out_id = jnp.arange(2 * rows, dtype=jnp.int32)
    wanted = out_id // (2 * per) * per + out_id % per
    side = out_id // per % 2
    from_row = jnp.sum(jnp.where((wanted // stripe)[:, None] == order[None, :], inverse[None, :], 0), axis=1)
    from_row = from_row * stripe + wanted % stripe
    pick = (from_row[:, None] == jnp.arange(rows, dtype=jnp.int32)[None, :])
    left = (pick & (side == 0)[:, None]).astype(bf16)
    right = (pick & (side == 1)[:, None]).astype(bf16)
    arranged = jnp.dot(
        jnp.concatenate([left, right], axis=1),
        jnp.concatenate([mixed[:, :half], mixed[:, half:width]], axis=0),
        preferred_element_type=f32,
    ).astype(bf16)
    mine = lax.all_to_all(arranged, ("x", "z"), split_axis=0, concat_axis=0, tiled=True)
    peers = lax.ppermute(mine, "c", swap)

    def spot(side, rel, s, src, i):
        part = (src != c).astype(jnp.int32)
        owner = jnp.where(rel == 0, c, 1 - c)
        return part * 2 * rows + s * 2 * per + side * per + owner * stripe + i

    idx = jnp.arange(nc * rows, dtype=jnp.int32)
    i_, src_, s_, rel_ = idx % stripe, idx // stripe % nc, idx // (stripe * nc) % chips, idx // rows
    wide_id = jnp.arange(2 * nc * rows, dtype=jnp.int32)
    low = wide_id % (nc * rows)
    where = spot(wide_id // (nc * rows), low // rows, low // (stripe * nc) % chips, low // stripe % nc, low % stripe)
    choose = (where[:, None] == wide_id[None, :]).astype(bf16)
    queries = jnp.dot(choose, jnp.concatenate([mine, peers], axis=0), preferred_element_type=f32).astype(bf16)
    owner_ = (x * nz + z) * nc + jnp.where(rel_ == 0, c, 1 - c)
    residue_ = jnp.sum(jnp.where(owner_[:, None] == order[None, :], inverse[None, :], 0), axis=1)
    natural = (s_ * nc + src_) * rows + residue_ * stripe + i_

    fresh = jnp.concatenate(
        [mixed[:, width : width + HEAD_SIZE], mixed[:, width + HEAD_SIZE :]], axis=0
    ).reshape(1, 2, rows, HEAD_SIZE)
    key_id = jnp.arange(nx * nz * rows, dtype=jnp.int32)
    key_x = jnp.where(key_id // (nz * rows) == 0, x, 1 - x)
    key_natural = ((key_x * nz + key_id // rows % nz) * nc + c) * rows + key_id % rows
    fresh_mask = jnp.where(key_natural[:, None] <= natural[None, :], 0.0, NEG).astype(bf16)

    slots = cached_key_rows.shape[0]

    def info_of(where):
        flip = jnp.array([w[0] for w in where], jnp.int32)
        step = jnp.array([w[1] + nz for w in where], jnp.int32)
        starts = ((jnp.where(flip == 0, x, 1 - x) * nz + (z + step) % nz) * nc + c) * slots
        return jnp.concatenate([prefix_len, starts.astype(jnp.int32)])

    def around(step):
        return [(0, -step), (1, -step), (0, step), (1, step)]

    two = 2 * slots
    near = ((0, 0), (0, two), (1, 0), (1, two), (2, 0), (2, two))
    pair = ((0, 0), (0, two), (1, 0), (1, two))
    fresh = jnp.broadcast_to(fresh, (nz, 2, rows, HEAD_SIZE))
    fresh = lax.all_to_all(fresh, "z", split_axis=0, concat_axis=0, tiled=True)
    first_info = info_of([(0, 0), (1, 0)] + around(1))
    state = attend(first_info, [both, up1, down1], near, queries, heads)
    up2, down2, fresh, state = lax.optimization_barrier((up2, down2, fresh, state))
    fresh_other = lax.ppermute(fresh, "x", swap)
    up3, down3 = hop(up2, down2)
    second_info = info_of(around(2))
    state = attend(second_info, [up2, down2], pair, queries, heads, state=state)
    up3, down3, state = lax.optimization_barrier((up3, down3, state))
    up4 = lax.ppermute(up3[:two], "z", up)
    down4 = lax.ppermute(down3[two:], "z", down)
    third_info = info_of(around(3))
    state = attend(third_info, [up3, down3], pair, queries, heads, state=state)
    keep, give, lse = attend(
        info_of([(0, 4), (1, 4)]),
        [up4, down4],
        ((0, 0), (1, 0)),
        queries,
        heads,
        fresh=(fresh, fresh_other, fresh_mask),
        state=state,
        last=True,
    )
    got = lax.ppermute(give, "c", swap)
    their_lse = lax.ppermute(lse, "c", swap)
    return merge(heads, keep, got, lse, their_lse)


def solution(mesh):
    devices = mesh.devices
    parts = Mesh(devices.reshape(2, devices.shape[0] // 4, 2, devices.shape[1]), ("x", "z", "c", "tp"))
    rows = ("x", "z", "c", "tp")
    cp = ("x", "z", "c")
    return jax.shard_map(
        step,
        mesh=parts,
        in_specs=(P(rows, None), P(rows, None), P(rows, None), P(cp, "tp"), P(cp, "tp"), P(), P()),
        out_specs=P(cp, "tp"),
        check_vma=False,
    )
```
